32 devices in a mesh: gx: 8 (over y, x, core), gy: 4 (over z).
Axes of the slice: x: 2, y: 2, z: 4, core: 2. Of those that a mesh axis runs over, the one named last changes fastest.
Arguments:
- positions: float32 [3, 8, 4, 32, 128], P(None, 'gx', 'gy'), may hold values from 0 to 1023, as said below
- counts: int32 [8, 4, 32], P('gx', 'gy'), may hold values from 16 to 128, as said below
- labels: int32 [8, 4, 32, 128], P('gx', 'gy'), may hold values from 0 to 5592404
Outputs:
- groups: int32 [8, 4, 32, 128], P('gx', 'gy')
The draws below stay inside these ranges and needn't reach their ends.
Inputs may be any that keep to these rules, and one draw needn't show every extreme that they name: `positions`: coordinates are whole numbers. `counts`: at least one cell holds 128 particles; slots at or beyond a cell's count are padding.
All inputs are finite; a program needn't handle non-finite values.
Results may differ from the reference program's by a relative error of at most 0.000001.
Values sent between devices are 32-bit elements; how exact they have to be, the bound alone decides.
A program may use at most 64 MiB of HBM per device.

```python
import jax
import jax.numpy as jnp
from jax import lax

SLOTS = 128
ITERS = 3
NX = 8
NY = 4
NZ = 32
LABEL_TOP = 5592405


def draw_positions(key, part):
    groups = max(2, SLOTS // 32)
    centres = jax.random.randint(jax.random.fold_in(key, 11), (3, NX, NY, NZ, groups), 0, 1024).astype(jnp.float32)
    corner_bits = jax.random.randint(jax.random.fold_in(key, 13), (3, NX, NY, NZ, groups), 0, 2).astype(jnp.float32) * 1023.0
    group_index = jnp.arange(groups)
    centres = jnp.where(group_index < 2, corner_bits, centres)
    member = jax.random.randint(jax.random.fold_in(key, 14), (NX, NY, NZ, SLOTS), 0, groups)
    member = jnp.broadcast_to(member[None], (3, NX, NY, NZ, SLOTS))
    placed = jnp.take_along_axis(centres, member, axis=4)
    spread_key = jax.random.fold_in(key, 12)
    jitter = jax.random.normal(spread_key, placed.shape, jnp.float32) * 24.0
    return jnp.clip(jnp.floor(placed + jitter), 0.0, 1023.0).astype(jnp.float32)


def draw_counts(key, part):
    drawn = jax.random.randint(jax.random.fold_in(key, 21), (NX, NY, NZ), max(1, SLOTS // 8), SLOTS + 1)
    chosen = jax.random.randint(jax.random.fold_in(key, 22), (), 0, NX * NY * NZ)
    flat_index = jnp.arange(NX * NY * NZ).reshape(NX, NY, NZ)
    return jnp.where(flat_index == chosen, SLOTS, drawn).astype(jnp.int32)


def touch_ends(values, rng, least, high):
    longest = values.shape.index(max(values.shape))
    spots = []
    for shift in (0, 1):
        where = [jax.random.randint(jax.random.fold_in(rng, axis), (), 0, length) for axis, length in enumerate(values.shape)]
        where[longest] = (where[longest] + shift) % values.shape[longest]
        spots.append(tuple(where))
    return values.at[spots[0]].set(least).at[spots[1]].set(high)


def setup_inputs(seed: int = 0) -> dict:
    key_list = jax.random.split(jax.random.key(seed), 4)
    return {
        "positions": draw_positions(jax.random.fold_in(key_list[3], 71), 0),
        "counts": draw_counts(jax.random.fold_in(key_list[3], 71), 0),
        "labels": touch_ends(jax.random.randint(key_list[2], (NX, NY, NZ, SLOTS), 0, LABEL_TOP), jax.random.fold_in(key_list[2], 1), 0, LABEL_TOP - 1).astype(jnp.int32),
    }


cell_side = 1024.0
link_square = 1040.0
ceiling = 16777216


def linked_minimum(own_points, near_points, near_labels, displace):
    squares = None
    for component in range(3):
        separation = (near_points[component][..., None, :] + displace[component]) - own_points[component][..., :, None]
        if squares is None:
            squares = separation * separation
        else:
            squares = squares + separation * separation
    joined = squares <= link_square
    return jnp.min(jnp.where(joined, near_labels[..., None, :], ceiling), axis=-1)


def reference(positions, counts, labels):
    slot_index = lax.broadcasted_iota(jnp.int32, labels.shape, 3)
    filled = slot_index < counts[..., None]
    current = jnp.where(filled, labels, ceiling).astype(jnp.int32)
    columns = jnp.moveaxis(positions, 1, 0)
    for sweep_index in range(ITERS):
        lowest = current
        for first_step in (-1, 0, 1):
            for second_step in (-1, 0, 1):
                for third_step in (-1, 0, 1):
                    moved = (-first_step, -second_step, -third_step)
                    near_points = jnp.moveaxis(jnp.roll(positions, moved, axis=(1, 2, 3)), 1, 0)
                    near_labels = jnp.roll(current, moved, axis=(0, 1, 2))
                    displace = (first_step * cell_side, second_step * cell_side, third_step * cell_side)

                    def visit(items, displace=displace):
                        return linked_minimum(items[0], items[1], items[2], displace)

                    nearest = lax.map(visit, (columns, near_points, near_labels))
                    lowest = jnp.minimum(lowest, nearest)
        current = jnp.where(filled, lowest, ceiling).astype(jnp.int32)
    return jnp.where(filled, current, -1).astype(jnp.int32)
```

```python
import itertools

import jax
import jax.numpy as jnp
from jax import lax
from jax.experimental import pallas as pl
from jax.experimental.pallas import tpu as pltpu
from jax.sharding import PartitionSpec as P

ITERS = 3

cell_side = 1024.0
link_square = 1040.0
sentinel = 16777216.0
middle = 512.0
reach = 64.0
step_row = 16
own_row = 24

MESH = pl.DeviceIdType.MESH

SUBSETS = [s for s in itertools.product((0, 1), repeat=3) if any(s)]
SUBSETS.sort(key=sum)
SIDES = {
    subset: list(itertools.product(*[(-1, 1) if crossed else (0,) for crossed in subset])) for subset in SUBSETS
}
BLOCKS = [sides for subset in SUBSETS for sides in SIDES[subset]]
COLUMNS = [c for c in itertools.product((-1, 0, 1), repeat=2) if c != (0, 0)]


def thirds(value):
    top = jnp.floor(value * (1.0 / 65536.0)) * 65536.0
    rest = value - top
    mid = jnp.floor(rest * (1.0 / 256.0)) * 256.0
    return [top, mid, rest - mid]


def halves(value):
    high = jnp.floor(value * (1.0 / 32.0)) * 32.0
    return high, value - high


def near_rows(points, sides):
    terms, norm = [], None
    for value, side in zip(points, sides):
        if side == 0:
            value = value - middle
            high, low = halves(value)
            terms += [high, low, high, low]
        else:
            value = jnp.minimum(value, reach) if side > 0 else jnp.maximum(value - cell_side, -reach)
            terms += [value]
        norm = value * value if norm is None else norm + value * value
    one = jnp.ones_like(norm)
    return thirds(norm) + [one, one, one] + terms


def own_rows(points, sides):
    terms, norm, chosen = [], None, None
    for value, side in zip(points, sides):
        if side == 0:
            value = value - middle
            high, low = halves(value)
            terms += [-2.0 * high, -2.0 * high, -2.0 * low, -2.0 * low]
        else:
            here = value >= middle if side > 0 else value < middle
            chosen = here if chosen is None else jnp.logical_and(chosen, here)
            value = jnp.maximum(value - cell_side, -reach) if side > 0 else jnp.minimum(value, reach)
            terms += [-2.0 * value]
        norm = value * value if norm is None else norm + value * value
    one = jnp.ones_like(norm)
    rows = [one, one, one] + thirds(norm - link_square) + terms
    scale = sentinel if chosen is None else jnp.where(chosen, sentinel, 0.0)
    return [row * scale for row in rows]


def put_rows(ref, rows, depth, size):
    zero = jnp.zeros_like(rows[0])
    for k in range(size):
        ref[pl.ds(k, depth, stride=size), :] = rows[k] if k < len(rows) else zero


def kernel(
    counts_ref, points_ref, labels_ref, groups_ref,
    halo_points, halo_labels, current, own_a, own_b, far_a, far_b, near_labels,
    turned0, turned1, turned2, turned3, gap,
    point_send, point_recv, label_send, label_recv,
):
    _, depth, slots = points_ref.shape
    gx, gy = lax.axis_size("gx"), lax.axis_size("gy")
    me_x, me_y = lax.axis_index("gx"), lax.axis_index("gy")

    def target(offset):
        return (lax.rem(me_x - offset[0] + gx, gx), lax.rem(me_y - offset[1] + gy, gy))

    barrier = pltpu.get_barrier_semaphore()
    for offset in COLUMNS:
        pl.semaphore_signal(barrier, inc=1, device_id=target(offset), device_id_type=MESH)

    slot = lax.broadcasted_iota(jnp.int32, (1, slots), 1)
    for e in range(depth):
        here = labels_ref[e : e + 1, :].astype(jnp.float32)
        current[0, e : e + 1, :] = jnp.where(slot < counts_ref[e], here, sentinel)

    pl.semaphore_wait(barrier, len(COLUMNS))

    def label_copies(step):
        return [
            pltpu.make_async_remote_copy(
                src_ref=current.at[step],
                dst_ref=halo_labels.at[step, n],
                send_sem=label_send.at[step, n],
                recv_sem=label_recv.at[step, n],
                device_id=target(offset),
                device_id_type=MESH,
            )
            for n, offset in enumerate(COLUMNS)
        ]

    point_copies = [
        pltpu.make_async_remote_copy(
            src_ref=points_ref,
            dst_ref=halo_points.at[n],
            send_sem=point_send.at[n],
            recv_sem=point_recv.at[n],
            device_id=target(offset),
            device_id_type=MESH,
        )
        for n, offset in enumerate(COLUMNS)
    ]
    for copy in point_copies:
        copy.start()
    copies = label_copies(0)
    for copy in copies:
        copy.start()

    own_points = [points_ref[k] for k in range(3)]
    put_rows(own_a, own_rows(own_points, (0, 0, 0)), depth, own_row)
    put_rows(own_b, near_rows(own_points, (0, 0, 0)), depth, own_row)
    for n, sides in enumerate(BLOCKS):
        put_rows(far_a.at[n], own_rows(own_points, sides), depth, step_row)
        if sides[:2] == (0, 0):
            put_rows(far_b.at[n], near_rows(own_points, sides), depth, step_row)

    turned = {1: turned1, 2: turned2, 3: turned3}
    place = {}
    for subset in SUBSETS:
        place[subset] = sum(1 for other in place if sum(other) == sum(subset))

    @pl.loop(0, depth)
    def _(e):
        at = pl.multiple_of(e * own_row, 8)
        turned0[e] = own_a[pl.ds(at, own_row), :].T.astype(jnp.bfloat16)
        at = pl.multiple_of(e * step_row, step_row)
        for subset in SUBSETS:
            rows = [far_a[BLOCKS.index(sides), pl.ds(at, step_row), :] for sides in SIDES[subset]]
            turned[sum(subset)][place[subset], e] = jnp.concatenate(rows, axis=0).T.astype(jnp.bfloat16)

    def put_labels(n, value):
        for k, row in enumerate(thirds(value)):
            near_labels[n, pl.ds(k, depth, stride=step_row), :] = row * (1.0 / sentinel)

    near_labels[...] = jnp.zeros_like(near_labels)

    for copy in point_copies:
        copy.wait_recv()
    for n, offset in enumerate(COLUMNS):
        points = [halo_points[n, k] for k in range(3)]
        for m, sides in enumerate(BLOCKS):
            if sides[:2] == offset:
                put_rows(far_b.at[m], near_rows(points, sides), depth, step_row)

    for step in range(ITERS):
        if step > 0:
            copies = label_copies(step)
            for copy in copies:
                copy.start()
        put_labels(len(COLUMNS), current[step])
        for copy in copies:
            copy.wait_recv()
        for n in range(len(COLUMNS)):
            put_labels(n, halo_labels[step, n])

        @pl.loop(0, depth)
        def _(e):
            spots = {
                0: pl.multiple_of(e * step_row, step_row),
                1: pl.multiple_of(lax.rem(e + 1, depth) * step_row, step_row),
                -1: pl.multiple_of(lax.rem(e + depth - 1, depth) * step_row, step_row),
            }
            own = current[step, pl.ds(e, 1), :]
            if step == 0:
                at = pl.multiple_of(e * own_row, 8)
                found = jnp.dot(
                    turned0[e],
                    own_b[pl.ds(at, own_row), :].astype(jnp.bfloat16),
                    preferred_element_type=jnp.float32,
                )
                gap[e, 0] = found
            else:
                found = gap[e, 0]
            least = jnp.maximum(found, own)
            for m, subset in enumerate(SUBSETS):
                sides_list = SIDES[subset]
                left = turned[sum(subset)][place[subset], e]
                columns = [COLUMNS.index(s[:2]) if s[:2] != (0, 0) else len(COLUMNS) for s in sides_list]
                right = jnp.concatenate(
                    [near_labels[c, pl.ds(spots[s[2]], step_row), :] for c, s in zip(columns, sides_list)], axis=0
                )
                if step == 0:
                    front = jnp.concatenate(
                        [far_b[BLOCKS.index(s), pl.ds(spots[s[2]], step_row), :] for s in sides_list], axis=0
                    )
                    both = jnp.concatenate([front, right], axis=1).astype(jnp.bfloat16)
                    result = jnp.dot(left, both, preferred_element_type=jnp.float32)
                    found, values = result[:, :slots], result[:, slots:]
                    gap[e, m + 1] = found
                else:
                    values = jnp.dot(left, right.astype(jnp.bfloat16), preferred_element_type=jnp.float32)
                    found = gap[e, m + 1]
                least = jnp.minimum(least, jnp.maximum(found, values))
            row = jnp.minimum(jnp.min(least.T, axis=0, keepdims=True), own)
            filled = slot < counts_ref[e]
            if step == ITERS - 1:
                groups_ref[pl.ds(e, 1), :] = jnp.where(filled, row, -1.0).astype(jnp.int32)
            else:
                current[step + 1, pl.ds(e, 1), :] = jnp.where(filled, row, sentinel)

        for copy in copies:
            copy.wait_send()
    for copy in point_copies:
        copy.wait_send()


def body(positions, counts, labels):
    depth, slots = positions.shape[3:]
    near = len(COLUMNS)
    groups = pl.pallas_call(
        kernel,
        out_shape=jax.ShapeDtypeStruct((depth, slots), jnp.int32),
        in_specs=[
            pl.BlockSpec(memory_space=pltpu.SMEM),
            pl.BlockSpec(memory_space=pltpu.VMEM),
            pl.BlockSpec(memory_space=pltpu.VMEM),
        ],
        out_specs=pl.BlockSpec(memory_space=pltpu.VMEM),
        scratch_shapes=[
            pltpu.VMEM((near, 3, depth, slots), jnp.float32),
            pltpu.VMEM((ITERS, near, depth, slots), jnp.float32),
            pltpu.VMEM((ITERS, depth, slots), jnp.float32),
            pltpu.VMEM((depth * own_row, slots), jnp.float32),
            pltpu.VMEM((depth * own_row, slots), jnp.float32),
            pltpu.VMEM((len(BLOCKS), depth * step_row, slots), jnp.float32),
            pltpu.VMEM((len(BLOCKS), depth * step_row, slots), jnp.float32),
            pltpu.VMEM((near + 1, depth * step_row, slots), jnp.float32),
            pltpu.VMEM((depth, slots, own_row), jnp.bfloat16),
            pltpu.VMEM((3, depth, slots, 2 * step_row), jnp.bfloat16),
            pltpu.VMEM((3, depth, slots, 4 * step_row), jnp.bfloat16),
            pltpu.VMEM((1, depth, slots, 8 * step_row), jnp.bfloat16),
            pltpu.VMEM((depth, len(SUBSETS) + 1, slots, slots), jnp.float32),
            pltpu.SemaphoreType.DMA((near,)),
            pltpu.SemaphoreType.DMA((near,)),
            pltpu.SemaphoreType.DMA((ITERS, near)),
            pltpu.SemaphoreType.DMA((ITERS, near)),
        ],
        compiler_params=pltpu.CompilerParams(
            collective_id=0, has_side_effects=True, vmem_limit_bytes=60 * 2**20
        ),
    )(counts.reshape(depth), positions.reshape(3, depth, slots), labels.reshape(depth, slots))
    return groups.reshape(labels.shape)


def solution(mesh):
    placed = (P(None, "gx", "gy", None, None), P("gx", "gy", None), P("gx", "gy", None, None))
    return jax.shard_map(
        body, mesh=mesh, in_specs=placed, out_specs=P("gx", "gy", None, None), check_vma=False
    )
```

```python
import itertools

import jax
import jax.numpy as jnp
from jax import lax
from jax.experimental import pallas as pl
from jax.experimental.pallas import tpu as pltpu
from jax.sharding import PartitionSpec as P

ITERS = 3

cell_side = 1024.0
link_square = 1040.0
sentinel = 16777216.0
middle = 512.0
reach = 64.0
step_row = 16
own_row = 24

MESH = pl.DeviceIdType.MESH

SUBSETS = [s for s in itertools.product((0, 1), repeat=3) if any(s)]
SUBSETS.sort(key=sum)
SIDES = {
    subset: list(itertools.product(*[(-1, 1) if crossed else (0,) for crossed in subset])) for subset in SUBSETS
}
BLOCKS = [sides for subset in SUBSETS for sides in SIDES[subset]]
COLUMNS = [c for c in itertools.product((-1, 0, 1), repeat=2) if c != (0, 0)]
COLUMNS.sort(key=lambda c: c[0] * c[0] + c[1] * c[1])


def thirds(value):
    top = jnp.floor(value * (1.0 / 65536.0)) * 65536.0
    rest = value - top
    mid = jnp.floor(rest * (1.0 / 256.0)) * 256.0
    return [top, mid, rest - mid]


def halves(value):
    high = jnp.floor(value * (1.0 / 32.0)) * 32.0
    return high, value - high


def block_size(crossed):
    return 8 if crossed == 3 else step_row


def near_rows(points, sides):
    terms, norm = [], None
    for value, side in zip(points, sides):
        if side == 0:
            value = value - middle
            high, low = halves(value)
            terms += [high, low, high, low]
        else:
            value = jnp.minimum(value, reach) if side > 0 else jnp.maximum(value - cell_side, -reach)
            terms += [value]
        norm = value * value if norm is None else norm + value * value
    crossed = sum(abs(side) for side in sides)
    ones = 2 if crossed == 3 else 3
    rows = dict(enumerate(thirds(norm)))
    if crossed == 3:
        del rows[0]
    rows.update((3 + ones + k, term) for k, term in enumerate(terms))
    return rows


def fixed_rows(sides, size, like):
    crossed = sum(abs(side) for side in sides)
    ones = 2 if crossed == 3 else 3
    terms = 3 + ones + sum(1 if side else 4 for side in sides)
    one, zero = jnp.ones_like(like), jnp.zeros_like(like)
    rows = {3 + k: one for k in range(ones)}
    rows.update((k, zero) for k in range(terms, size))
    if crossed == 3:
        rows[0] = zero
    return rows


def own_rows(points, subset, size):
    terms, norm = [], None
    for value, crossed in zip(points, subset):
        if crossed:
            value = jnp.where(
                value >= middle, jnp.maximum(value - cell_side, -reach), jnp.minimum(value, reach)
            )
            terms += [-2.0 * value]
        else:
            value = value - middle
            high, low = halves(value)
            terms += [-2.0 * high, -2.0 * high, -2.0 * low, -2.0 * low]
        norm = value * value if norm is None else norm + value * value
    one = jnp.ones_like(norm)
    norm = norm - link_square
    if sum(subset) == 3:
        mid = jnp.floor(norm * (1.0 / 256.0)) * 256.0
        split = [mid, norm - mid]
    else:
        split = thirds(norm)
    rows = [one, one, one] + split + terms
    rows += [jnp.zeros_like(norm)] * (size - len(rows))
    return dict(enumerate(rows))


def put_rows(ref, rows, depth, size):
    for k, row in rows.items():
        ref[pl.ds(k, depth, stride=size), :] = row


def kernel(
    counts_ref, points_ref, labels_ref, groups_ref,
    halo_points, halo_labels, current, own_a, own_b, side_a, hot, far_b, corner_b, near_labels,
    turned0, turned1, turned2, turned3, gap,
    point_send, point_recv, label_send, label_recv,
):
    _, depth, slots = points_ref.shape
    gx, gy = lax.axis_size("gx"), lax.axis_size("gy")
    me_x, me_y = lax.axis_index("gx"), lax.axis_index("gy")

    def target(offset):
        return (lax.rem(me_x - offset[0] + gx, gx), lax.rem(me_y - offset[1] + gy, gy))

    barrier = pltpu.get_barrier_semaphore()
    for offset in COLUMNS:
        pl.semaphore_signal(barrier, inc=1, device_id=target(offset), device_id_type=MESH)

    slot = lax.broadcasted_iota(jnp.int32, (1, slots), 1)
    for e in range(depth):
        here = labels_ref[e : e + 1, :].astype(jnp.float32)
        current[0, e : e + 1, :] = jnp.where(slot < counts_ref[e], here, sentinel)

    pl.semaphore_wait(barrier, len(COLUMNS))

    def label_copies(step):
        return [
            pltpu.make_async_remote_copy(
                src_ref=current.at[step],
                dst_ref=halo_labels.at[step, n],
                send_sem=label_send.at[step, n],
                recv_sem=label_recv.at[step, n],
                device_id=target(offset),
                device_id_type=MESH,
            )
            for n, offset in enumerate(COLUMNS)
        ]

    point_copies = [
        pltpu.make_async_remote_copy(
            src_ref=points_ref,
            dst_ref=halo_points.at[n],
            send_sem=point_send.at[n],
            recv_sem=point_recv.at[n],
            device_id=target(offset),
            device_id_type=MESH,
        )
        for n, offset in enumerate(COLUMNS)
    ]
    for copy in point_copies:
        copy.start()
    copies = label_copies(0)
    for copy in copies:
        copy.start()

    own_points = [points_ref[k] for k in range(3)]

    def near_block(sides):
        if all(sides):
            return corner_b.at[BLOCKS.index(sides) - len(BLOCKS) + 8]
        return far_b.at[BLOCKS.index(sides)]

    put_rows(own_a, own_rows(own_points, (0, 0, 0), own_row), depth, own_row)
    for m, subset in enumerate(SUBSETS):
        put_rows(side_a.at[m], own_rows(own_points, subset, block_size(sum(subset))), depth, block_size(sum(subset)))
    upper = [value >= middle for value in own_points]
    for n, sides in enumerate(BLOCKS):
        chosen = None
        for high, side in zip(upper, sides):
            if side:
                here = high if side > 0 else jnp.logical_not(high)
                chosen = here if chosen is None else jnp.logical_and(chosen, here)
        hot[n] = jnp.where(chosen, sentinel, 0.0)

    turned = {1: turned1, 2: turned2, 3: turned3}
    place = {}
    for subset in SUBSETS:
        place[subset] = sum(1 for other in place if sum(other) == sum(subset))

    @pl.loop(0, depth, unroll=2)
    def _(e):
        at = pl.multiple_of(e * own_row, 8)
        turned0[e] = (own_a[pl.ds(at, own_row), :] * sentinel).T.astype(jnp.bfloat16)
        for m, subset in enumerate(SUBSETS):
            size = block_size(sum(subset))
            base = side_a[m, pl.ds(pl.multiple_of(e * size, size), size), :]
            rows = [base * hot[BLOCKS.index(sides), pl.ds(e, 1), :] for sides in SIDES[subset]]
            turned[sum(subset)][place[subset], e] = jnp.concatenate(rows, axis=0).T.astype(jnp.bfloat16)

    like = own_points[0]
    put_rows(own_b, fixed_rows((0, 0, 0), own_row, like), depth, own_row)
    put_rows(own_b, near_rows(own_points, (0, 0, 0)), depth, own_row)
    for sides in BLOCKS:
        size = block_size(sum(abs(side) for side in sides))
        put_rows(near_block(sides), fixed_rows(sides, size, like), depth, size)
        if sides[:2] == (0, 0):
            put_rows(near_block(sides), near_rows(own_points, sides), depth, size)

    def put_labels(n, value):
        for k, row in enumerate(thirds(value)):
            near_labels[n, pl.ds(k, depth, stride=step_row), :] = row * (1.0 / sentinel)

    near_labels[...] = jnp.zeros_like(near_labels)

    for n, offset in enumerate(COLUMNS):
        point_copies[n].wait_recv()
        points = [halo_points[n, k] for k in range(3)]
        for sides in BLOCKS:
            if sides[:2] == offset:
                size = block_size(sum(abs(side) for side in sides))
                put_rows(near_block(sides), near_rows(points, sides), depth, size)

    for step in range(ITERS):
        if step > 0:
            copies = label_copies(step)
            for copy in copies:
                copy.start()
        put_labels(len(COLUMNS), current[step])
        for copy in copies:
            copy.wait_recv()
        for n in range(len(COLUMNS)):
            put_labels(n, halo_labels[step, n])

        @pl.loop(0, depth, unroll=2)
        def _(e):
            cells = {0: e, 1: lax.rem(e + 1, depth), -1: lax.rem(e + depth - 1, depth)}

            def spot(side, stride, size):
                return pl.ds(pl.multiple_of(cells[side] * stride, size), size)

            own = current[step, pl.ds(e, 1), :]
            if step == 0:
                at = pl.multiple_of(e * own_row, 8)
                found = jnp.dot(
                    turned0[e],
                    own_b[pl.ds(at, own_row), :].astype(jnp.bfloat16),
                    preferred_element_type=jnp.float32,
                )
                gap[e, 0] = found
            else:
                found = gap[e, 0]
            least = jnp.maximum(found, own)
            for m, subset in enumerate(SUBSETS):
                sides_list = SIDES[subset]
                left = turned[sum(subset)][place[subset], e]
                columns = [COLUMNS.index(s[:2]) if s[:2] != (0, 0) else len(COLUMNS) for s in sides_list]
                size = block_size(sum(subset))
                right = jnp.concatenate(
                    [near_labels[c, spot(s[2], step_row, size), :] for c, s in zip(columns, sides_list)], axis=0
                )
                if step == 0:
                    front = jnp.concatenate(
                        [near_block(s)[spot(s[2], size, size), :] for s in sides_list], axis=0
                    )
                    both = jnp.concatenate([front, right], axis=1).astype(jnp.bfloat16)
                    result = jnp.dot(left, both, preferred_element_type=jnp.float32)
                    found, values = result[:, :slots], result[:, slots:]
                    gap[e, m + 1] = found
                else:
                    values = jnp.dot(left, right.astype(jnp.bfloat16), preferred_element_type=jnp.float32)
                    found = gap[e, m + 1]
                least = jnp.minimum(least, jnp.maximum(found, values))
            row = jnp.minimum(jnp.min(least.T, axis=0, keepdims=True), own)
            filled = slot < counts_ref[e]
            if step == ITERS - 1:
                groups_ref[pl.ds(e, 1), :] = jnp.where(filled, row, -1.0).astype(jnp.int32)
            else:
                current[step + 1, pl.ds(e, 1), :] = jnp.where(filled, row, sentinel)

        for copy in copies:
            copy.wait_send()
    for copy in point_copies:
        copy.wait_send()


def body(positions, counts, labels):
    depth, slots = positions.shape[3:]
    near = len(COLUMNS)
    groups = pl.pallas_call(
        kernel,
        out_shape=jax.ShapeDtypeStruct((depth, slots), jnp.int32),
        in_specs=[
            pl.BlockSpec(memory_space=pltpu.SMEM),
            pl.BlockSpec(memory_space=pltpu.VMEM),
            pl.BlockSpec(memory_space=pltpu.VMEM),
        ],
        out_specs=pl.BlockSpec(memory_space=pltpu.VMEM),
        scratch_shapes=[
            pltpu.VMEM((near, 3, depth, slots), jnp.float32),
            pltpu.VMEM((ITERS, near, depth, slots), jnp.float32),
            pltpu.VMEM((ITERS, depth, slots), jnp.float32),
            pltpu.VMEM((depth * own_row, slots), jnp.float32),
            pltpu.VMEM((depth * own_row, slots), jnp.float32),
            pltpu.VMEM((len(SUBSETS), depth * step_row, slots), jnp.float32),
            pltpu.VMEM((len(BLOCKS), depth, slots), jnp.float32),
            pltpu.VMEM((len(BLOCKS) - 8, depth * step_row, slots), jnp.float32),
            pltpu.VMEM((8, depth * 8, slots), jnp.float32),
            pltpu.VMEM((near + 1, depth * step_row, slots), jnp.float32),
            pltpu.VMEM((depth, slots, own_row), jnp.bfloat16),
            pltpu.VMEM((3, depth, slots, 2 * step_row), jnp.bfloat16),
            pltpu.VMEM((3, depth, slots, 4 * step_row), jnp.bfloat16),
            pltpu.VMEM((1, depth, slots, 8 * 8), jnp.bfloat16),
            pltpu.VMEM((depth, len(SUBSETS) + 1, slots, slots), jnp.float32),
            pltpu.SemaphoreType.DMA((near,)),
            pltpu.SemaphoreType.DMA((near,)),
            pltpu.SemaphoreType.DMA((ITERS, near)),
            pltpu.SemaphoreType.DMA((ITERS, near)),
        ],
        compiler_params=pltpu.CompilerParams(
            collective_id=0, has_side_effects=True, vmem_limit_bytes=60 * 2**20
        ),
    )(counts.reshape(depth), positions.reshape(3, depth, slots), labels.reshape(depth, slots))
    return groups.reshape(labels.shape)


def solution(mesh):
    placed = (P(None, "gx", "gy", None, None), P("gx", "gy", None), P("gx", "gy", None, None))
    return jax.shard_map(
        body, mesh=mesh, in_specs=placed, out_specs=P("gx", "gy", None, None), check_vma=False
    )
```

```python
import itertools

import jax
import jax.numpy as jnp
from jax import lax
from jax.experimental import pallas as pl
from jax.experimental.pallas import tpu as pltpu
from jax.sharding import PartitionSpec as P

ITERS = 3

cell_side = 1024.0
link_square = 1040.0
sentinel = 16777216.0
middle = 512.0
reach = 64.0
step_row = 16
own_row = 32

MESH = pl.DeviceIdType.MESH

SUBSETS = [s for s in itertools.product((0, 1), repeat=3) if any(s)]
SUBSETS.sort(key=sum)
SIDES = {
    subset: list(itertools.product(*[(-1, 1) if crossed else (0,) for crossed in subset])) for subset in SUBSETS
}
BLOCKS = [sides for subset in SUBSETS for sides in SIDES[subset]]
COLUMNS = [(-1, 0), (1, 0), (0, -1), (0, 1), (-1, -1), (-1, 1), (1, -1), (1, 1)]

PHASES = [
    (((0, 0, 0), (0, 0, 1)), ()),
    (((1, 0, 0), (1, 0, 1)), (0, 1)),
    (((0, 1, 0), (0, 1, 1)), (2, 3)),
    (((1, 1, 0), (1, 1, 1)), (4, 5, 6, 7)),
]


def thirds(value):
    top = jnp.floor(value * (1.0 / 65536.0)) * 65536.0
    rest = value - top
    mid = jnp.floor(rest * (1.0 / 256.0)) * 256.0
    return [top, mid, rest - mid]


def halves(value):
    high = jnp.floor(value * (1.0 / 32.0)) * 32.0
    return high, value - high


def block_size(crossed):
    return 8 if crossed == 3 else step_row


def near_rows(points, sides):
    terms, norm = [], None
    for value, side in zip(points, sides):
        if side == 0:
            value = value - middle
            high, low = halves(value)
            terms += [high, low, high, low]
        else:
            value = jnp.minimum(value, reach) if side > 0 else jnp.maximum(value - cell_side, -reach)
            terms += [value]
        norm = value * value if norm is None else norm + value * value
    crossed = sum(abs(side) for side in sides)
    ones = 2 if crossed == 3 else 3
    rows = dict(enumerate(thirds(norm)))
    if crossed == 3:
        del rows[0]
    rows.update((3 + ones + k, term) for k, term in enumerate(terms))
    return rows


def fixed_rows(sides, size, like):
    crossed = sum(abs(side) for side in sides)
    ones = 2 if crossed == 3 else 3
    terms = 3 + ones + sum(1 if side else 4 for side in sides)
    one, zero = jnp.ones_like(like), jnp.zeros_like(like)
    rows = {3 + k: one for k in range(ones)}
    rows.update((k, zero) for k in range(terms, size))
    if crossed == 3:
        rows[0] = zero
    return rows


def own_rows(points, subset, size):
    terms, norm = [], None
    for value, crossed in zip(points, subset):
        if crossed:
            value = jnp.where(
                value >= middle, jnp.maximum(value - cell_side, -reach), jnp.minimum(value, reach)
            )
            terms += [-2.0 * value]
        else:
            value = value - middle
            high, low = halves(value)
            terms += [-2.0 * high, -2.0 * high, -2.0 * low, -2.0 * low]
        norm = value * value if norm is None else norm + value * value
    one = jnp.ones_like(norm)
    norm = norm - link_square
    if sum(subset) == 3:
        mid = jnp.floor(norm * (1.0 / 256.0)) * 256.0
        split = [mid, norm - mid]
    else:
        split = thirds(norm)
    rows = [one, one, one] + split + terms
    rows += [jnp.zeros_like(norm)] * (size - len(rows))
    return dict(enumerate(rows))


def put_rows(ref, rows, depth, size):
    for k, row in rows.items():
        ref[pl.ds(k, depth, stride=size), :] = row


def kernel(
    counts_ref, points_ref, labels_ref, groups_ref,
    halo_points, halo_labels, current, own_a, own_b, side_a, hot, far_b, corner_b, near_labels,
    turned0, turned1, turned2, turned3, gap, lowest,
    point_send, point_recv, label_send, label_recv,
):
    _, depth, slots = points_ref.shape
    gx, gy = lax.axis_size("gx"), lax.axis_size("gy")
    me_x, me_y = lax.axis_index("gx"), lax.axis_index("gy")

    def target(offset):
        return (lax.rem(me_x - offset[0] + gx, gx), lax.rem(me_y - offset[1] + gy, gy))

    barrier = pltpu.get_barrier_semaphore()
    for offset in COLUMNS:
        pl.semaphore_signal(barrier, inc=1, device_id=target(offset), device_id_type=MESH)

    slot = lax.broadcasted_iota(jnp.int32, (1, slots), 1)
    for e in range(depth):
        here = labels_ref[e : e + 1, :].astype(jnp.float32)
        current[0, e : e + 1, :] = jnp.where(slot < counts_ref[e], here, sentinel)

    pl.semaphore_wait(barrier, len(COLUMNS))

    def label_copies(step):
        return [
            pltpu.make_async_remote_copy(
                src_ref=current.at[step],
                dst_ref=halo_labels.at[step, n],
                send_sem=label_send.at[step, n],
                recv_sem=label_recv.at[step, n],
                device_id=target(offset),
                device_id_type=MESH,
            )
            for n, offset in enumerate(COLUMNS)
        ]

    point_copies = [
        pltpu.make_async_remote_copy(
            src_ref=points_ref,
            dst_ref=halo_points.at[n],
            send_sem=point_send.at[n],
            recv_sem=point_recv.at[n],
            device_id=target(offset),
            device_id_type=MESH,
        )
        for n, offset in enumerate(COLUMNS)
    ]
    copies = label_copies(0)
    for point_copy, label_copy in zip(point_copies, copies):
        point_copy.start()
        label_copy.start()

    own_points = [points_ref[k] for k in range(3)]

    def near_block(sides):
        if all(sides):
            return corner_b.at[BLOCKS.index(sides) - len(BLOCKS) + 8]
        return far_b.at[BLOCKS.index(sides)]

    put_rows(own_a, own_rows(own_points, (0, 0, 0), own_row), depth, own_row)
    for m, subset in enumerate(SUBSETS):
        put_rows(side_a.at[m], own_rows(own_points, subset, block_size(sum(subset))), depth, block_size(sum(subset)))
    upper = [value >= middle for value in own_points]
    for n, sides in enumerate(BLOCKS):
        chosen = None
        for high, side in zip(upper, sides):
            if side:
                here = high if side > 0 else jnp.logical_not(high)
                chosen = here if chosen is None else jnp.logical_and(chosen, here)
        hot[n] = jnp.where(chosen, sentinel, 0.0)

    turned = (turned0, turned1, turned2, turned3)

    @pl.loop(0, depth, unroll=2)
    def _(e):
        for phase, (subsets, _) in enumerate(PHASES):
            rows = []
            for subset in subsets:
                if not any(subset):
                    rows.append(own_a[pl.ds(pl.multiple_of(e * own_row, own_row), own_row), :] * sentinel)
                    continue
                size = block_size(sum(subset))
                base = side_a[SUBSETS.index(subset), pl.ds(pl.multiple_of(e * size, size), size), :]
                rows += [base * hot[BLOCKS.index(sides), pl.ds(e, 1), :] for sides in SIDES[subset]]
            turned[phase][e] = jnp.concatenate(rows, axis=0).T.astype(jnp.bfloat16)

    like = own_points[0]
    put_rows(own_b, fixed_rows((0, 0, 0), own_row, like), depth, own_row)
    put_rows(own_b, near_rows(own_points, (0, 0, 0)), depth, own_row)
    for sides in BLOCKS:
        size = block_size(sum(abs(side) for side in sides))
        put_rows(near_block(sides), fixed_rows(sides, size, like), depth, size)
        if sides[:2] == (0, 0):
            put_rows(near_block(sides), near_rows(own_points, sides), depth, size)

    def put_labels(n, value):
        for k, row in enumerate(thirds(value)):
            near_labels[n, pl.ds(k, depth, stride=step_row), :] = row * (1.0 / sentinel)

    near_labels[...] = jnp.zeros_like(near_labels)

    def diagonal(first, second):
        top = jnp.concatenate([first, jnp.zeros((first.shape[0], second.shape[1]), first.dtype)], axis=1)
        low = jnp.concatenate([jnp.zeros((second.shape[0], first.shape[1]), first.dtype), second], axis=1)
        return jnp.concatenate([top, low], axis=0)

    def sweep(step, phase, subsets):
        last = phase == len(PHASES) - 1

        @pl.loop(0, depth, unroll=4)
        def _(e):
            cells = {0: e, 1: lax.rem(e + 1, depth), -1: lax.rem(e + depth - 1, depth)}

            def spot(side, stride, size):
                return pl.ds(pl.multiple_of(cells[side] * stride, size), size)

            def label_rows(subset):
                rows = []
                for sides in SIDES[subset]:
                    column = COLUMNS.index(sides[:2]) if any(sides[:2]) else len(COLUMNS)
                    rows.append(near_labels[column, spot(sides[2], step_row, block_size(sum(subset))), :])
                return jnp.concatenate(rows, axis=0)

            def gap_rows(subset):
                if not any(subset):
                    return own_b[spot(0, own_row, own_row), :]
                size = block_size(sum(subset))
                return jnp.concatenate([near_block(s)[spot(s[2], size, size), :] for s in SIDES[subset]], axis=0)

            def product(right):
                return jnp.dot(turned[phase][e], right.astype(jnp.bfloat16), preferred_element_type=jnp.float32)

            own = current[step, pl.ds(e, 1), :]
            if step == 0:
                found = product(diagonal(gap_rows(subsets[0]), gap_rows(subsets[1])))
                gap[e, phase] = found
            else:
                found = gap[e, phase]
            second = label_rows(subsets[1])
            if phase == 0:
                values = product(jnp.concatenate([jnp.zeros((own_row, slots), jnp.float32), second], axis=0))
                least = jnp.minimum(jnp.maximum(found[:, :slots], own), jnp.maximum(found[:, slots:], values))
            else:
                values = product(diagonal(label_rows(subsets[0]), second))
                either = jnp.maximum(found, values)
                least = jnp.minimum(lowest[e], jnp.minimum(either[:, :slots], either[:, slots:]))
            if not last:
                lowest[e] = least
                return
            row = jnp.minimum(jnp.min(least.T, axis=0, keepdims=True), own)
            filled = slot < counts_ref[e]
            if step == ITERS - 1:
                groups_ref[pl.ds(e, 1), :] = jnp.where(filled, row, -1.0).astype(jnp.int32)
            else:
                current[step + 1, pl.ds(e, 1), :] = jnp.where(filled, row, sentinel)

    for step in range(ITERS):
        if step > 0:
            copies = label_copies(step)
            for copy in copies:
                copy.start()
        put_labels(len(COLUMNS), current[step])
        for phase, (subsets, columns) in enumerate(PHASES):
            for n in columns:
                if step == 0:
                    point_copies[n].wait_recv()
                    points = [halo_points[n, k] for k in range(3)]
                    for sides in BLOCKS:
                        if sides[:2] == COLUMNS[n]:
                            size = block_size(sum(abs(side) for side in sides))
                            put_rows(near_block(sides), near_rows(points, sides), depth, size)
                copies[n].wait_recv()
                put_labels(n, halo_labels[step, n])
            sweep(step, phase, subsets)
        for copy in copies:
            copy.wait_send()
    for copy in point_copies:
        copy.wait_send()


def body(positions, counts, labels):
    depth, slots = positions.shape[3:]
    near = len(COLUMNS)
    groups = pl.pallas_call(
        kernel,
        out_shape=jax.ShapeDtypeStruct((depth, slots), jnp.int32),
        in_specs=[
            pl.BlockSpec(memory_space=pltpu.SMEM),
            pl.BlockSpec(memory_space=pltpu.VMEM),
            pl.BlockSpec(memory_space=pltpu.VMEM),
        ],
        out_specs=pl.BlockSpec(memory_space=pltpu.VMEM),
        scratch_shapes=[
            pltpu.VMEM((near, 3, depth, slots), jnp.float32),
            pltpu.VMEM((ITERS, near, depth, slots), jnp.float32),
            pltpu.VMEM((ITERS, depth, slots), jnp.float32),
            pltpu.VMEM((depth * own_row, slots), jnp.float32),
            pltpu.VMEM((depth * own_row, slots), jnp.float32),
            pltpu.VMEM((len(SUBSETS), depth * step_row, slots), jnp.float32),
            pltpu.VMEM((len(BLOCKS), depth, slots), jnp.float32),
            pltpu.VMEM((len(BLOCKS) - 8, depth * step_row, slots), jnp.float32),
            pltpu.VMEM((8, depth * 8, slots), jnp.float32),
            pltpu.VMEM((near + 1, depth * step_row, slots), jnp.float32),
            pltpu.VMEM((depth, slots, own_row + 2 * step_row), jnp.bfloat16),
            pltpu.VMEM((depth, slots, 6 * step_row), jnp.bfloat16),
            pltpu.VMEM((depth, slots, 6 * step_row), jnp.bfloat16),
            pltpu.VMEM((depth, slots, 8 * step_row), jnp.bfloat16),
            pltpu.VMEM((depth, len(PHASES), slots, 2 * slots), jnp.float32),
            pltpu.VMEM((depth, slots, slots), jnp.float32),
            pltpu.SemaphoreType.DMA((near,)),
            pltpu.SemaphoreType.DMA((near,)),
            pltpu.SemaphoreType.DMA((ITERS, near)),
            pltpu.SemaphoreType.DMA((ITERS, near)),
        ],
        compiler_params=pltpu.CompilerParams(
            collective_id=0, has_side_effects=True, vmem_limit_bytes=60 * 2**20
        ),
    )(counts.reshape(depth), positions.reshape(3, depth, slots), labels.reshape(depth, slots))
    return groups.reshape(labels.shape)


def solution(mesh):
    placed = (P(None, "gx", "gy", None, None), P("gx", "gy", None), P("gx", "gy", None, None))
    return jax.shard_map(
        body, mesh=mesh, in_specs=placed, out_specs=P("gx", "gy", None, None), check_vma=False
    )
```

```python
import itertools

import jax
import jax.numpy as jnp
from jax import lax
from jax.experimental import pallas as pl
from jax.experimental.pallas import tpu as pltpu
from jax.sharding import PartitionSpec as P

ITERS = 3

cell_side = 1024.0
link_square = 1040.0
sentinel = 16777216.0
middle = 512.0
reach = 64.0
step_row = 16
head_row = 8
own_row = 32

MESH = pl.DeviceIdType.MESH

SUBSETS = [s for s in itertools.product((0, 1), repeat=3) if any(s)]
SUBSETS.sort(key=sum)
SIDES = {
    subset: list(itertools.product(*[(-1, 1) if crossed else (0,) for crossed in subset])) for subset in SUBSETS
}
BLOCKS = [sides for subset in SUBSETS for sides in SIDES[subset]]
COLUMNS = [(-1, 0), (1, 0), (0, -1), (0, 1), (-1, -1), (-1, 1), (1, -1), (1, 1)]

PHASES = [
    (((0, 0, 0), (0, 0, 1)), ()),
    (((1, 0, 0), (1, 0, 1)), (0, 1)),
    (((0, 1, 0), (0, 1, 1)), (2, 3)),
    (((1, 1, 0), (1, 1, 1)), (4, 5, 6, 7)),
]


def thirds(value):
    top = jnp.floor(value * (1.0 / 65536.0)) * 65536.0
    rest = value - top
    mid = jnp.floor(rest * (1.0 / 256.0)) * 256.0
    return [top, mid, rest - mid]


def halves(value):
    high = jnp.floor(value * (1.0 / 32.0)) * 32.0
    return high, value - high


def block_size(crossed):
    return 8 if crossed == 3 else step_row


def near_rows(points, sides):
    terms, norm = [], None
    for value, side in zip(points, sides):
        if side == 0:
            value = value - middle
            high, low = halves(value)
            terms += [high, low, high, low]
        else:
            value = jnp.minimum(value, reach) if side > 0 else jnp.maximum(value - cell_side, -reach)
            terms += [value]
        norm = value * value if norm is None else norm + value * value
    crossed = sum(abs(side) for side in sides)
    ones = 2 if crossed == 3 else 3
    rows = dict(enumerate(thirds(norm)))
    if crossed == 3:
        del rows[0]
    rows.update((3 + ones + k, term) for k, term in enumerate(terms))
    return rows


def fixed_rows(sides, size, like):
    crossed = sum(abs(side) for side in sides)
    ones = 2 if crossed == 3 else 3
    terms = 3 + ones + sum(1 if side else 4 for side in sides)
    one, zero = jnp.ones_like(like), jnp.zeros_like(like)
    rows = {3 + k: one for k in range(ones)}
    rows.update((k, zero) for k in range(terms, size))
    if crossed == 3:
        rows[0] = zero
    return rows


def own_rows(points, subset, size):
    terms, norm = [], None
    for value, crossed in zip(points, subset):
        if crossed:
            value = jnp.where(
                value >= middle, jnp.maximum(value - cell_side, -reach), jnp.minimum(value, reach)
            )
            terms += [-2.0 * value]
        else:
            value = value - middle
            high, low = halves(value)
            terms += [-2.0 * high, -2.0 * high, -2.0 * low, -2.0 * low]
        norm = value * value if norm is None else norm + value * value
    one = jnp.ones_like(norm)
    norm = norm - link_square
    if sum(subset) == 3:
        mid = jnp.floor(norm * (1.0 / 256.0)) * 256.0
        split = [mid, norm - mid]
    else:
        split = thirds(norm)
    rows = [one, one, one] + split + terms
    rows += [jnp.zeros_like(norm)] * (size - len(rows))
    return dict(enumerate(rows))


def put_rows(ref, rows, depth, size):
    for k, row in rows.items():
        ref[pl.ds(k, depth, stride=size), :] = row


def kernel(
    counts_ref, points_ref, labels_ref, groups_ref,
    halo_points, halo_labels, current, own_a, own_b, side_a, hot, far_b, corner_b, near_labels,
    turned0, turned1, turned2, turned3, gap, lowest,
    point_send, point_recv, label_send, label_recv,
):
    _, depth, slots = points_ref.shape
    gx, gy = lax.axis_size("gx"), lax.axis_size("gy")
    me_x, me_y = lax.axis_index("gx"), lax.axis_index("gy")

    def target(offset):
        return (lax.rem(me_x - offset[0] + gx, gx), lax.rem(me_y - offset[1] + gy, gy))

    barrier = pltpu.get_barrier_semaphore()
    for offset in COLUMNS:
        pl.semaphore_signal(barrier, inc=1, device_id=target(offset), device_id_type=MESH)

    slot = lax.broadcasted_iota(jnp.int32, (1, slots), 1)
    for e in range(depth):
        here = labels_ref[e : e + 1, :].astype(jnp.float32)
        current[0, e : e + 1, :] = jnp.where(slot < counts_ref[e], here, sentinel)

    pl.semaphore_wait(barrier, len(COLUMNS))

    def label_copies(step):
        return [
            pltpu.make_async_remote_copy(
                src_ref=current.at[step],
                dst_ref=halo_labels.at[step, n],
                send_sem=label_send.at[step, n],
                recv_sem=label_recv.at[step, n],
                device_id=target(offset),
                device_id_type=MESH,
            )
            for n, offset in enumerate(COLUMNS)
        ]

    point_copies = [
        pltpu.make_async_remote_copy(
            src_ref=points_ref,
            dst_ref=halo_points.at[n],
            send_sem=point_send.at[n],
            recv_sem=point_recv.at[n],
            device_id=target(offset),
            device_id_type=MESH,
        )
        for n, offset in enumerate(COLUMNS)
    ]
    copies = label_copies(0)
    for point_copy, label_copy in zip(point_copies, copies):
        point_copy.start()
        label_copy.start()

    own_points = [points_ref[k] for k in range(3)]

    def near_block(sides):
        if all(sides):
            return corner_b.at[BLOCKS.index(sides) - len(BLOCKS) + 8]
        return far_b.at[BLOCKS.index(sides)]

    put_rows(own_a, own_rows(own_points, (0, 0, 0), own_row), depth, own_row)
    for m, subset in enumerate(SUBSETS):
        put_rows(side_a.at[m], own_rows(own_points, subset, block_size(sum(subset))), depth, block_size(sum(subset)))
    upper = [value >= middle for value in own_points]
    for n, sides in enumerate(BLOCKS):
        chosen = None
        for high, side in zip(upper, sides):
            if side:
                here = high if side > 0 else jnp.logical_not(high)
                chosen = here if chosen is None else jnp.logical_and(chosen, here)
        hot[n] = jnp.where(chosen, sentinel, 0.0)

    turned = (turned0, turned1, turned2, turned3)

    @pl.loop(0, depth, unroll=4)
    def _(e):
        for phase, (subsets, _) in enumerate(PHASES):
            heads, tails = [], []
            for subset in subsets:
                if not any(subset):
                    continue
                size = block_size(sum(subset))
                base = side_a[SUBSETS.index(subset), pl.ds(pl.multiple_of(e * size, size), size), :]
                for sides in SIDES[subset]:
                    chosen = hot[BLOCKS.index(sides), pl.ds(e, 1), :]
                    heads.append(base[:head_row] * chosen)
                    if size > head_row:
                        tails.append(base[head_row:] * chosen)
            if phase == 0:
                tails.append(own_a[pl.ds(pl.multiple_of(e * own_row, own_row), own_row), :] * sentinel)
            rows = heads + tails
            turned[phase][e] = jnp.concatenate(rows, axis=0).T.astype(jnp.bfloat16)

    like = own_points[0]
    put_rows(own_b, fixed_rows((0, 0, 0), own_row, like), depth, own_row)
    put_rows(own_b, near_rows(own_points, (0, 0, 0)), depth, own_row)
    for sides in BLOCKS:
        size = block_size(sum(abs(side) for side in sides))
        put_rows(near_block(sides), fixed_rows(sides, size, like), depth, size)
        if sides[:2] == (0, 0):
            put_rows(near_block(sides), near_rows(own_points, sides), depth, size)

    def put_labels(n, value):
        for k, row in enumerate(thirds(value)):
            near_labels[n, pl.ds(k, depth, stride=head_row), :] = row * (1.0 / sentinel)

    near_labels[...] = jnp.zeros_like(near_labels)

    def wide(block, half):
        blank = jnp.zeros_like(block)
        return jnp.concatenate([blank, block] if half else [block, blank], axis=1)

    def sweep(step, phase, subsets):
        last = phase == len(PHASES) - 1

        @pl.loop(0, depth, unroll=8)
        def _(e):
            cells = {0: e, 1: lax.rem(e + 1, depth), -1: lax.rem(e + depth - 1, depth)}

            def spot(side, stride, size):
                return pl.ds(pl.multiple_of(cells[side] * stride, size), size)

            def label_rows(subset):
                rows = []
                for sides in SIDES[subset]:
                    column = COLUMNS.index(sides[:2]) if any(sides[:2]) else len(COLUMNS)
                    rows.append(near_labels[column, spot(sides[2], head_row, head_row), :])
                return jnp.concatenate(rows, axis=0)

            def gap_rows():
                heads, tails = [], []
                for half, subset in enumerate(subsets):
                    if not any(subset):
                        continue
                    size = block_size(sum(subset))
                    for sides in SIDES[subset]:
                        block = near_block(sides)[spot(sides[2], size, size), :]
                        heads.append(wide(block[:head_row], half))
                        if size > head_row:
                            tails.append(wide(block[head_row:], half))
                if phase == 0:
                    tails.append(wide(own_b[spot(0, own_row, own_row), :], 0))
                return jnp.concatenate(heads + tails, axis=0)

            left = turned[phase][e]

            def product(right):
                return jnp.dot(
                    left[:, : right.shape[0]], right.astype(jnp.bfloat16), preferred_element_type=jnp.float32
                )

            own = current[step, pl.ds(e, 1), :]
            if step == 0:
                found = product(gap_rows())
                gap[e, phase] = found
            else:
                found = gap[e, phase]
            second = label_rows(subsets[1])
            if phase == 0:
                values = product(second)
                least = jnp.minimum(jnp.maximum(found[:, :slots], own), jnp.maximum(found[:, slots:], values))
            else:
                values = product(jnp.concatenate([wide(label_rows(subsets[0]), 0), wide(second, 1)], axis=0))
                either = jnp.maximum(found, values)
                least = jnp.minimum(lowest[e], jnp.minimum(either[:, :slots], either[:, slots:]))
            if not last:
                lowest[e] = least
                return
            row = jnp.minimum(jnp.min(least.T, axis=0, keepdims=True), own)
            filled = slot < counts_ref[e]
            if step == ITERS - 1:
                groups_ref[pl.ds(e, 1), :] = jnp.where(filled, row, -1.0).astype(jnp.int32)
            else:
                current[step + 1, pl.ds(e, 1), :] = jnp.where(filled, row, sentinel)

    for step in range(ITERS):
        if step > 0:
            copies = label_copies(step)
            for copy in copies:
                copy.start()
        put_labels(len(COLUMNS), current[step])
        for phase, (subsets, columns) in enumerate(PHASES):
            for n in columns:
                if step == 0:
                    point_copies[n].wait_recv()
                    points = [halo_points[n, k] for k in range(3)]
                    for sides in BLOCKS:
                        if sides[:2] == COLUMNS[n]:
                            size = block_size(sum(abs(side) for side in sides))
                            put_rows(near_block(sides), near_rows(points, sides), depth, size)
                copies[n].wait_recv()
                put_labels(n, halo_labels[step, n])
            sweep(step, phase, subsets)
        for copy in copies:
            copy.wait_send()
    for copy in point_copies:
        copy.wait_send()


def body(positions, counts, labels):
    depth, slots = positions.shape[3:]
    near = len(COLUMNS)
    groups = pl.pallas_call(
        kernel,
        out_shape=jax.ShapeDtypeStruct((depth, slots), jnp.int32),
        in_specs=[
            pl.BlockSpec(memory_space=pltpu.SMEM),
            pl.BlockSpec(memory_space=pltpu.VMEM),
            pl.BlockSpec(memory_space=pltpu.VMEM),
        ],
        out_specs=pl.BlockSpec(memory_space=pltpu.VMEM),
        scratch_shapes=[
            pltpu.VMEM((near, 3, depth, slots), jnp.float32),
            pltpu.VMEM((ITERS, near, depth, slots), jnp.float32),
            pltpu.VMEM((ITERS, depth, slots), jnp.float32),
            pltpu.VMEM((depth * own_row, slots), jnp.float32),
            pltpu.VMEM((depth * own_row, slots), jnp.float32),
            pltpu.VMEM((len(SUBSETS), depth * step_row, slots), jnp.float32),
            pltpu.VMEM((len(BLOCKS), depth, slots), jnp.float32),
            pltpu.VMEM((len(BLOCKS) - 8, depth * step_row, slots), jnp.float32),
            pltpu.VMEM((8, depth * 8, slots), jnp.float32),
            pltpu.VMEM((near + 1, depth * head_row, slots), jnp.float32),
            pltpu.VMEM((depth, slots, own_row + 2 * step_row), jnp.bfloat16),
            pltpu.VMEM((depth, slots, 6 * step_row), jnp.bfloat16),
            pltpu.VMEM((depth, slots, 6 * step_row), jnp.bfloat16),
            pltpu.VMEM((depth, slots, 8 * step_row), jnp.bfloat16),
            pltpu.VMEM((depth, len(PHASES), slots, 2 * slots), jnp.float32),
            pltpu.VMEM((depth, slots, slots), jnp.float32),
            pltpu.SemaphoreType.DMA((near,)),
            pltpu.SemaphoreType.DMA((near,)),
            pltpu.SemaphoreType.DMA((ITERS, near)),
            pltpu.SemaphoreType.DMA((ITERS, near)),
        ],
        compiler_params=pltpu.CompilerParams(
            collective_id=0, has_side_effects=True, vmem_limit_bytes=60 * 2**20
        ),
    )(counts.reshape(depth), positions.reshape(3, depth, slots), labels.reshape(depth, slots))
    return groups.reshape(labels.shape)


def solution(mesh):
    placed = (P(None, "gx", "gy", None, None), P("gx", "gy", None), P("gx", "gy", None, None))
    return jax.shard_map(
        body, mesh=mesh, in_specs=placed, out_specs=P("gx", "gy", None, None), check_vma=False
    )
```

```python
import itertools

import jax
import jax.numpy as jnp
from jax import lax
from jax.experimental import pallas as pl
from jax.experimental.pallas import tpu as pltpu
from jax.sharding import PartitionSpec as P

ITERS = 3

cell_side = 1024.0
link_square = 1040.0
sentinel = 16777216.0
middle = 512.0
reach = 64.0
step_row = 16
head_row = 8
own_row = 32

MESH = pl.DeviceIdType.MESH

SUBSETS = [s for s in itertools.product((0, 1), repeat=3) if any(s)]
SUBSETS.sort(key=sum)
SIDES = {
    subset: list(itertools.product(*[(-1, 1) if crossed else (0,) for crossed in subset])) for subset in SUBSETS
}
BLOCKS = [sides for subset in SUBSETS for sides in SIDES[subset]]
COLUMNS = [(-1, 0), (1, 0), (0, -1), (0, 1), (-1, -1), (-1, 1), (1, -1), (1, 1)]

PHASES = [
    (((0, 0, 0), (0, 0, 1)), ()),
    (((1, 0, 0), (1, 0, 1)), (0, 1)),
    (((0, 1, 0), (0, 1, 1)), (2, 3)),
    (((1, 1, 0), (1, 1, 1)), (4, 5, 6, 7)),
]


def thirds(value):
    top = jnp.floor(value * (1.0 / 65536.0)) * 65536.0
    rest = value - top
    mid = jnp.floor(rest * (1.0 / 256.0)) * 256.0
    return [top, mid, rest - mid]


def halves(value):
    high = jnp.floor(value * (1.0 / 32.0)) * 32.0
    return high, value - high


def block_size(crossed):
    return 8 if crossed == 3 else step_row


def near_rows(points, sides):
    terms, norm = [], None
    for value, side in zip(points, sides):
        if side == 0:
            value = value - middle
            high, low = halves(value)
            terms += [high, low, high, low]
        else:
            value = jnp.minimum(value, reach) if side > 0 else jnp.maximum(value - cell_side, -reach)
            terms += [value]
        norm = value * value if norm is None else norm + value * value
    crossed = sum(abs(side) for side in sides)
    ones = 2 if crossed == 3 else 3
    rows = dict(enumerate(thirds(norm)))
    if crossed == 3:
        del rows[0]
    rows.update((3 + ones + k, term) for k, term in enumerate(terms))
    return rows


def fixed_rows(sides, size, like):
    crossed = sum(abs(side) for side in sides)
    ones = 2 if crossed == 3 else 3
    terms = 3 + ones + sum(1 if side else 4 for side in sides)
    one, zero = jnp.ones_like(like), jnp.zeros_like(like)
    rows = {3 + k: one for k in range(ones)}
    rows.update((k, zero) for k in range(terms, size))
    if crossed == 3:
        rows[0] = zero
    return rows


def own_rows(points, subset, size):
    terms, norm = [], None
    for value, crossed in zip(points, subset):
        if crossed:
            value = jnp.where(
                value >= middle, jnp.maximum(value - cell_side, -reach), jnp.minimum(value, reach)
            )
            terms += [-2.0 * value]
        else:
            value = value - middle
            high, low = halves(value)
            terms += [-2.0 * high, -2.0 * high, -2.0 * low, -2.0 * low]
        norm = value * value if norm is None else norm + value * value
    one = jnp.ones_like(norm)
    norm = norm - link_square
    if sum(subset) == 3:
        mid = jnp.floor(norm * (1.0 / 256.0)) * 256.0
        split = [mid, norm - mid]
    else:
        split = thirds(norm)
    rows = [one, one, one] + split + terms
    rows += [jnp.zeros_like(norm)] * (size - len(rows))
    return dict(enumerate(rows))


def put_rows(ref, rows, depth, size):
    for k, row in rows.items():
        ref[pl.ds(k, depth, stride=size), :] = row


def kernel(
    counts_ref, points_ref, labels_ref, groups_ref,
    halo_points, halo_labels, current, own_a, own_b, side_a, hot, far_b, corner_b, near_labels,
    turned0, turned1, turned2, turned3, gap, lowest,
    point_send, point_recv, label_send, label_recv,
):
    _, depth, slots = points_ref.shape
    gx, gy = lax.axis_size("gx"), lax.axis_size("gy")
    me_x, me_y = lax.axis_index("gx"), lax.axis_index("gy")

    def target(offset):
        return (lax.rem(me_x - offset[0] + gx, gx), lax.rem(me_y - offset[1] + gy, gy))

    barrier = pltpu.get_barrier_semaphore()
    for offset in COLUMNS:
        pl.semaphore_signal(barrier, inc=1, device_id=target(offset), device_id_type=MESH)

    slot = lax.broadcasted_iota(jnp.int32, (1, slots), 1)
    for e in range(depth):
        here = labels_ref[e : e + 1, :].astype(jnp.float32)
        current[0, e : e + 1, :] = jnp.where(slot < counts_ref[e], here, sentinel)

    def label_copies(step):
        return [
            pltpu.make_async_remote_copy(
                src_ref=current.at[step],
                dst_ref=halo_labels.at[step, n],
                send_sem=label_send.at[step, n],
                recv_sem=label_recv.at[step, n],
                device_id=target(offset),
                device_id_type=MESH,
            )
            for n, offset in enumerate(COLUMNS)
        ]

    point_copies = [
        pltpu.make_async_remote_copy(
            src_ref=points_ref,
            dst_ref=halo_points.at[n],
            send_sem=point_send.at[n],
            recv_sem=point_recv.at[n],
            device_id=target(offset),
            device_id_type=MESH,
        )
        for n, offset in enumerate(COLUMNS)
    ]
    own_points = [points_ref[k] for k in range(3)]

    def near_block(sides):
        if all(sides):
            return corner_b.at[BLOCKS.index(sides) - len(BLOCKS) + 8]
        return far_b.at[BLOCKS.index(sides)]

    put_rows(own_a, own_rows(own_points, (0, 0, 0), own_row), depth, own_row)
    for m, subset in enumerate(SUBSETS):
        put_rows(side_a.at[m], own_rows(own_points, subset, block_size(sum(subset))), depth, block_size(sum(subset)))
    upper = [value >= middle for value in own_points]
    for n, sides in enumerate(BLOCKS):
        chosen = None
        for high, side in zip(upper, sides):
            if side:
                here = high if side > 0 else jnp.logical_not(high)
                chosen = here if chosen is None else jnp.logical_and(chosen, here)
        hot[n] = jnp.where(chosen, sentinel, 0.0)

    pl.semaphore_wait(barrier, len(COLUMNS))
    copies = label_copies(0)
    for point_copy, label_copy in zip(point_copies, copies):
        point_copy.start()
        label_copy.start()

    turned = (turned0, turned1, turned2, turned3)

    @pl.loop(0, depth, unroll=4)
    def _(e):
        for phase, (subsets, _) in enumerate(PHASES):
            heads, tails = [], []
            for subset in subsets:
                if not any(subset):
                    continue
                size = block_size(sum(subset))
                base = side_a[SUBSETS.index(subset), pl.ds(pl.multiple_of(e * size, size), size), :]
                for sides in SIDES[subset]:
                    chosen = hot[BLOCKS.index(sides), pl.ds(e, 1), :]
                    heads.append(base[:head_row] * chosen)
                    if size > head_row:
                        tails.append(base[head_row:] * chosen)
            if phase == 0:
                tails.append(own_a[pl.ds(pl.multiple_of(e * own_row, own_row), own_row), :] * sentinel)
            rows = heads + tails
            turned[phase][e] = jnp.concatenate(rows, axis=0).astype(jnp.bfloat16).T

    like = own_points[0]
    put_rows(own_b, fixed_rows((0, 0, 0), own_row, like), depth, own_row)
    put_rows(own_b, near_rows(own_points, (0, 0, 0)), depth, own_row)
    for sides in BLOCKS:
        size = block_size(sum(abs(side) for side in sides))
        put_rows(near_block(sides), fixed_rows(sides, size, like), depth, size)
        if sides[:2] == (0, 0):
            put_rows(near_block(sides), near_rows(own_points, sides), depth, size)

    def put_labels(n, value):
        for k, row in enumerate(thirds(value)):
            near_labels[n, pl.ds(k, depth, stride=head_row), :] = row * (1.0 / sentinel)

    near_labels[...] = jnp.zeros_like(near_labels)

    def wide(block, half):
        blank = jnp.zeros_like(block)
        return jnp.concatenate([blank, block] if half else [block, blank], axis=1)

    def sweep(step, phase, subsets):
        last = phase == len(PHASES) - 1

        @pl.loop(0, depth, unroll=16)
        def _(e):
            cells = {0: e, 1: lax.rem(e + 1, depth), -1: lax.rem(e + depth - 1, depth)}

            def spot(side, stride, size):
                return pl.ds(pl.multiple_of(cells[side] * stride, size), size)

            def label_rows(subset):
                rows = []
                for sides in SIDES[subset]:
                    column = COLUMNS.index(sides[:2]) if any(sides[:2]) else len(COLUMNS)
                    rows.append(near_labels[column, spot(sides[2], head_row, head_row), :])
                return jnp.concatenate(rows, axis=0)

            def gap_rows():
                heads, tails = [], []
                for half, subset in enumerate(subsets):
                    if not any(subset):
                        continue
                    size = block_size(sum(subset))
                    for sides in SIDES[subset]:
                        block = near_block(sides)[spot(sides[2], size, size), :]
                        heads.append(wide(block[:head_row], half))
                        if size > head_row:
                            tails.append(wide(block[head_row:], half))
                if phase == 0:
                    tails.append(wide(own_b[spot(0, own_row, own_row), :], 0))
                return jnp.concatenate(heads + tails, axis=0)

            left = turned[phase][e]

            def product(right):
                return jnp.dot(
                    left[:, : right.shape[0]], right.astype(jnp.bfloat16), preferred_element_type=jnp.float32
                )

            own = current[step, pl.ds(e, 1), :]
            if step == 0:
                found = product(gap_rows())
                gap[e, phase] = found
            else:
                found = gap[e, phase]
            second = label_rows(subsets[1])
            if phase == 0:
                values = product(second)
                least = jnp.minimum(jnp.maximum(found[:, :slots], own), jnp.maximum(found[:, slots:], values))
            else:
                values = product(jnp.concatenate([wide(label_rows(subsets[0]), 0), wide(second, 1)], axis=0))
                either = jnp.maximum(found, values)
                least = jnp.minimum(lowest[e], jnp.minimum(either[:, :slots], either[:, slots:]))
            if not last:
                lowest[e] = least
                return
            row = jnp.minimum(jnp.min(least.T, axis=0, keepdims=True), own)
            filled = slot < counts_ref[e]
            if step == ITERS - 1:
                groups_ref[pl.ds(e, 1), :] = jnp.where(filled, row, -1.0).astype(jnp.int32)
            else:
                current[step + 1, pl.ds(e, 1), :] = jnp.where(filled, row, sentinel)

    for step in range(ITERS):
        if step > 0:
            copies = label_copies(step)
            for copy in copies:
                copy.start()
        put_labels(len(COLUMNS), current[step])
        for phase, (subsets, columns) in enumerate(PHASES):
            for n in columns:
                if step == 0:
                    point_copies[n].wait_recv()
                    points = [halo_points[n, k] for k in range(3)]
                    for sides in BLOCKS:
                        if sides[:2] == COLUMNS[n]:
                            size = block_size(sum(abs(side) for side in sides))
                            put_rows(near_block(sides), near_rows(points, sides), depth, size)
                copies[n].wait_recv()
                put_labels(n, halo_labels[step, n])
            sweep(step, phase, subsets)
        for copy in copies:
            copy.wait_send()
    for copy in point_copies:
        copy.wait_send()


def body(positions, counts, labels):
    depth, slots = positions.shape[3:]
    near = len(COLUMNS)
    groups = pl.pallas_call(
        kernel,
        out_shape=jax.ShapeDtypeStruct((depth, slots), jnp.int32),
        in_specs=[
            pl.BlockSpec(memory_space=pltpu.SMEM),
            pl.BlockSpec(memory_space=pltpu.VMEM),
            pl.BlockSpec(memory_space=pltpu.VMEM),
        ],
        out_specs=pl.BlockSpec(memory_space=pltpu.VMEM),
        scratch_shapes=[
            pltpu.VMEM((near, 3, depth, slots), jnp.float32),
            pltpu.VMEM((ITERS, near, depth, slots), jnp.float32),
            pltpu.VMEM((ITERS, depth, slots), jnp.float32),
            pltpu.VMEM((depth * own_row, slots), jnp.float32),
            pltpu.VMEM((depth * own_row, slots), jnp.float32),
            pltpu.VMEM((len(SUBSETS), depth * step_row, slots), jnp.float32),
            pltpu.VMEM((len(BLOCKS), depth, slots), jnp.float32),
            pltpu.VMEM((len(BLOCKS) - 8, depth * step_row, slots), jnp.float32),
            pltpu.VMEM((8, depth * 8, slots), jnp.float32),
            pltpu.VMEM((near + 1, depth * head_row, slots), jnp.float32),
            pltpu.VMEM((depth, slots, own_row + 2 * step_row), jnp.bfloat16),
            pltpu.VMEM((depth, slots, 6 * step_row), jnp.bfloat16),
            pltpu.VMEM((depth, slots, 6 * step_row), jnp.bfloat16),
            pltpu.VMEM((depth, slots, 8 * step_row), jnp.bfloat16),
            pltpu.VMEM((depth, len(PHASES), slots, 2 * slots), jnp.float32),
            pltpu.VMEM((depth, slots, slots), jnp.float32),
            pltpu.SemaphoreType.DMA((near,)),
            pltpu.SemaphoreType.DMA((near,)),
            pltpu.SemaphoreType.DMA((ITERS, near)),
            pltpu.SemaphoreType.DMA((ITERS, near)),
        ],
        compiler_params=pltpu.CompilerParams(
            collective_id=0, has_side_effects=True, vmem_limit_bytes=60 * 2**20
        ),
    )(counts.reshape(depth), positions.reshape(3, depth, slots), labels.reshape(depth, slots))
    return groups.reshape(labels.shape)


def solution(mesh):
    placed = (P(None, "gx", "gy", None, None), P("gx", "gy", None), P("gx", "gy", None, None))
    return jax.shard_map(
        body, mesh=mesh, in_specs=placed, out_specs=P("gx", "gy", None, None), check_vma=False
    )
```

```python
import itertools

import jax
import jax.numpy as jnp
from jax import lax
from jax.experimental import pallas as pl
from jax.experimental.pallas import tpu as pltpu
from jax.sharding import PartitionSpec as P

ITERS = 3

cell_side = 1024.0
link_square = 1040.0
sentinel = 16777216.0
middle = 512.0
reach = 64.0
step_row = 16
head_row = 8
own_row = 32

MESH = pl.DeviceIdType.MESH

SUBSETS = [s for s in itertools.product((0, 1), repeat=3) if any(s)]
SUBSETS.sort(key=sum)
SIDES = {
    subset: list(itertools.product(*[(-1, 1) if crossed else (0,) for crossed in subset])) for subset in SUBSETS
}
BLOCKS = [sides for subset in SUBSETS for sides in SIDES[subset]]
COLUMNS = [(-1, 0), (1, 0), (0, -1), (0, 1), (-1, -1), (-1, 1), (1, -1), (1, 1)]

PHASES = [
    (((0, 0, 0), (0, 0, 1)), ()),
    (((1, 0, 0), (1, 0, 1)), (0, 1)),
    (((0, 1, 0), (0, 1, 1)), (2, 3)),
    (((1, 1, 0), (1, 1, 1)), (4, 5, 6, 7)),
]


def thirds(value):
    top = jnp.floor(value * (1.0 / 65536.0)) * 65536.0
    rest = value - top
    mid = jnp.floor(rest * (1.0 / 256.0)) * 256.0
    return [top, mid, rest - mid]


def halves(value):
    high = jnp.floor(value * (1.0 / 32.0)) * 32.0
    return high, value - high


def block_size(crossed):
    return 8 if crossed == 3 else step_row


def near_rows(points, sides):
    terms, norm = [], None
    for value, side in zip(points, sides):
        if side == 0:
            value = value - middle
            high, low = halves(value)
            terms += [high, low, high, low]
        else:
            value = jnp.minimum(value, reach) if side > 0 else jnp.maximum(value - cell_side, -reach)
            terms += [value]
        norm = value * value if norm is None else norm + value * value
    crossed = sum(abs(side) for side in sides)
    ones = 2 if crossed == 3 else 3
    rows = dict(enumerate(thirds(norm)))
    if crossed == 3:
        del rows[0]
    rows.update((3 + ones + k, term) for k, term in enumerate(terms))
    return rows


def fixed_rows(sides, size, like):
    crossed = sum(abs(side) for side in sides)
    ones = 2 if crossed == 3 else 3
    terms = 3 + ones + sum(1 if side else 4 for side in sides)
    one, zero = jnp.ones_like(like), jnp.zeros_like(like)
    rows = {3 + k: one for k in range(ones)}
    rows.update((k, zero) for k in range(terms, size))
    if crossed == 3:
        rows[0] = zero
    return rows


def own_rows(points, subset, size):
    terms, norm = [], None
    for value, crossed in zip(points, subset):
        if crossed:
            value = jnp.where(
                value >= middle, jnp.maximum(value - cell_side, -reach), jnp.minimum(value, reach)
            )
            terms += [-2.0 * value]
        else:
            value = value - middle
            high, low = halves(value)
            terms += [-2.0 * high, -2.0 * high, -2.0 * low, -2.0 * low]
        norm = value * value if norm is None else norm + value * value
    one = jnp.ones_like(norm)
    norm = norm - link_square
    if sum(subset) == 3:
        mid = jnp.floor(norm * (1.0 / 256.0)) * 256.0
        split = [mid, norm - mid]
    else:
        split = thirds(norm)
    rows = [one, one, one] + split + terms
    rows += [jnp.zeros_like(norm)] * (size - len(rows))
    return dict(enumerate(rows))


def put_rows(ref, rows, depth, size):
    for k, row in rows.items():
        ref[pl.ds(k, depth, stride=size), :] = row


def kernel(
    counts_ref, points_ref, labels_ref, groups_ref,
    halo_points, halo_labels, current, own_a, own_b, side_a, hot, far_b, corner_b, near_labels,
    turned0, turned1, turned2, turned3, gap, lowest,
    point_send, point_recv, label_send, label_recv,
):
    _, depth, slots = points_ref.shape
    gx, gy = lax.axis_size("gx"), lax.axis_size("gy")
    me_x, me_y = lax.axis_index("gx"), lax.axis_index("gy")

    def target(offset):
        return (lax.rem(me_x - offset[0] + gx, gx), lax.rem(me_y - offset[1] + gy, gy))

    barrier = pltpu.get_barrier_semaphore()
    for offset in COLUMNS:
        pl.semaphore_signal(barrier, inc=1, device_id=target(offset), device_id_type=MESH)

    slot = lax.broadcasted_iota(jnp.int32, (1, slots), 1)
    for e in range(depth):
        here = labels_ref[e : e + 1, :].astype(jnp.float32)
        current[0, e : e + 1, :] = jnp.where(slot < counts_ref[e], here, sentinel)

    def label_copies(step):
        return [
            pltpu.make_async_remote_copy(
                src_ref=current.at[step],
                dst_ref=halo_labels.at[step, n],
                send_sem=label_send.at[step, n],
                recv_sem=label_recv.at[step, n],
                device_id=target(offset),
                device_id_type=MESH,
            )
            for n, offset in enumerate(COLUMNS)
        ]

    point_copies = [
        pltpu.make_async_remote_copy(
            src_ref=halo_points.at[COLUMNS.index((0, offset[1]))] if all(offset) else points_ref,
            dst_ref=halo_points.at[n],
            send_sem=point_send.at[n],
            recv_sem=point_recv.at[n],
            device_id=target((offset[0], 0) if all(offset) else offset),
            device_id_type=MESH,
        )
        for n, offset in enumerate(COLUMNS)
    ]
    own_points = [points_ref[k] for k in range(3)]

    def near_block(sides):
        if all(sides):
            return corner_b.at[BLOCKS.index(sides) - len(BLOCKS) + 8]
        return far_b.at[BLOCKS.index(sides)]

    put_rows(own_a, own_rows(own_points, (0, 0, 0), own_row), depth, own_row)
    for m, subset in enumerate(SUBSETS):
        put_rows(side_a.at[m], own_rows(own_points, subset, block_size(sum(subset))), depth, block_size(sum(subset)))
    upper = [value >= middle for value in own_points]
    for n, sides in enumerate(BLOCKS):
        chosen = None
        for high, side in zip(upper, sides):
            if side:
                here = high if side > 0 else jnp.logical_not(high)
                chosen = here if chosen is None else jnp.logical_and(chosen, here)
        hot[n] = jnp.where(chosen, sentinel, 0.0)

    pl.semaphore_wait(barrier, len(COLUMNS))
    copies = label_copies(0)
    for n, label_copy in enumerate(copies):
        if not all(COLUMNS[n]):
            point_copies[n].start()
        label_copy.start()

    turned = (turned0, turned1, turned2, turned3)

    @pl.loop(0, depth, unroll=4)
    def _(e):
        for phase, (subsets, _) in enumerate(PHASES):
            heads, tails = [], []
            for subset in subsets:
                if not any(subset):
                    continue
                size = block_size(sum(subset))
                base = side_a[SUBSETS.index(subset), pl.ds(pl.multiple_of(e * size, size), size), :]
                for sides in SIDES[subset]:
                    chosen = hot[BLOCKS.index(sides), pl.ds(e, 1), :]
                    heads.append(base[:head_row] * chosen)
                    if size > head_row:
                        tails.append(base[head_row:] * chosen)
            if phase == 0:
                tails.append(own_a[pl.ds(pl.multiple_of(e * own_row, own_row), own_row), :] * sentinel)
            rows = heads + tails
            turned[phase][e] = jnp.concatenate(rows, axis=0).astype(jnp.bfloat16).T

    like = own_points[0]
    put_rows(own_b, fixed_rows((0, 0, 0), own_row, like), depth, own_row)
    put_rows(own_b, near_rows(own_points, (0, 0, 0)), depth, own_row)
    for sides in BLOCKS:
        size = block_size(sum(abs(side) for side in sides))
        put_rows(near_block(sides), fixed_rows(sides, size, like), depth, size)
        if sides[:2] == (0, 0):
            put_rows(near_block(sides), near_rows(own_points, sides), depth, size)

    def put_labels(n, value):
        for k, row in enumerate(thirds(value)):
            near_labels[n, pl.ds(k, depth, stride=head_row), :] = row * (1.0 / sentinel)

    near_labels[...] = jnp.zeros_like(near_labels)

    def wide(block, half):
        blank = jnp.zeros_like(block)
        return jnp.concatenate([blank, block] if half else [block, blank], axis=1)

    def sweep(step, phase, subsets):
        last = phase == len(PHASES) - 1

        @pl.loop(0, depth, unroll=16)
        def _(e):
            cells = {0: e, 1: lax.rem(e + 1, depth), -1: lax.rem(e + depth - 1, depth)}

            def spot(side, stride, size):
                return pl.ds(pl.multiple_of(cells[side] * stride, size), size)

            def label_rows(subset):
                rows = []
                for sides in SIDES[subset]:
                    column = COLUMNS.index(sides[:2]) if any(sides[:2]) else len(COLUMNS)
                    rows.append(near_labels[column, spot(sides[2], head_row, head_row), :])
                return jnp.concatenate(rows, axis=0)

            def gap_rows():
                heads, tails = [], []
                for half, subset in enumerate(subsets):
                    if not any(subset):
                        continue
                    size = block_size(sum(subset))
                    for sides in SIDES[subset]:
                        block = near_block(sides)[spot(sides[2], size, size), :]
                        heads.append(wide(block[:head_row], half))
                        if size > head_row:
                            tails.append(wide(block[head_row:], half))
                if phase == 0:
                    tails.append(wide(own_b[spot(0, own_row, own_row), :], 0))
                return jnp.concatenate(heads + tails, axis=0)

            left = turned[phase][e]

            def product(right):
                return jnp.dot(
                    left[:, : right.shape[0]], right.astype(jnp.bfloat16), preferred_element_type=jnp.float32
                )

            own = current[step, pl.ds(e, 1), :]
            if step == 0:
                found = product(gap_rows())
                gap[e, phase] = found
            else:
                found = gap[e, phase]
            second = label_rows(subsets[1])
            if phase == 0:
                values = product(second)
                least = jnp.minimum(jnp.maximum(found[:, :slots], own), jnp.maximum(found[:, slots:], values))
            else:
                values = product(jnp.concatenate([wide(label_rows(subsets[0]), 0), wide(second, 1)], axis=0))
                either = jnp.maximum(found, values)
                least = jnp.minimum(lowest[e], jnp.minimum(either[:, :slots], either[:, slots:]))
            if not last:
                lowest[e] = least
                return
            row = jnp.minimum(jnp.min(least.T, axis=0, keepdims=True), own)
            filled = slot < counts_ref[e]
            if step == ITERS - 1:
                groups_ref[pl.ds(e, 1), :] = jnp.where(filled, row, -1.0).astype(jnp.int32)
            else:
                current[step + 1, pl.ds(e, 1), :] = jnp.where(filled, row, sentinel)

    for n in (2, 3):
        point_copies[n].wait_recv()
    for n in (4, 5, 6, 7):
        point_copies[n].start()

    for step in range(ITERS):
        if step > 0:
            copies = label_copies(step)
            for copy in copies:
                copy.start()
        put_labels(len(COLUMNS), current[step])
        for phase, (subsets, columns) in enumerate(PHASES):
            for n in columns:
                if step == 0:
                    if n not in (2, 3):
                        point_copies[n].wait_recv()
                    points = [halo_points[n, k] for k in range(3)]
                    for sides in BLOCKS:
                        if sides[:2] == COLUMNS[n]:
                            size = block_size(sum(abs(side) for side in sides))
                            put_rows(near_block(sides), near_rows(points, sides), depth, size)
                copies[n].wait_recv()
                put_labels(n, halo_labels[step, n])
            sweep(step, phase, subsets)
        for copy in copies:
            copy.wait_send()
    for copy in point_copies:
        copy.wait_send()


def body(positions, counts, labels):
    depth, slots = positions.shape[3:]
    near = len(COLUMNS)
    groups = pl.pallas_call(
        kernel,
        out_shape=jax.ShapeDtypeStruct((depth, slots), jnp.int32),
        in_specs=[
            pl.BlockSpec(memory_space=pltpu.SMEM),
            pl.BlockSpec(memory_space=pltpu.VMEM),
            pl.BlockSpec(memory_space=pltpu.VMEM),
        ],
        out_specs=pl.BlockSpec(memory_space=pltpu.VMEM),
        scratch_shapes=[
            pltpu.VMEM((near, 3, depth, slots), jnp.float32),
            pltpu.VMEM((ITERS, near, depth, slots), jnp.float32),
            pltpu.VMEM((ITERS, depth, slots), jnp.float32),
            pltpu.VMEM((depth * own_row, slots), jnp.float32),
            pltpu.VMEM((depth * own_row, slots), jnp.float32),
            pltpu.VMEM((len(SUBSETS), depth * step_row, slots), jnp.float32),
            pltpu.VMEM((len(BLOCKS), depth, slots), jnp.float32),
            pltpu.VMEM((len(BLOCKS) - 8, depth * step_row, slots), jnp.float32),
            pltpu.VMEM((8, depth * 8, slots), jnp.float32),
            pltpu.VMEM((near + 1, depth * head_row, slots), jnp.float32),
            pltpu.VMEM((depth, slots, own_row + 2 * step_row), jnp.bfloat16),
            pltpu.VMEM((depth, slots, 6 * step_row), jnp.bfloat16),
            pltpu.VMEM((depth, slots, 6 * step_row), jnp.bfloat16),
            pltpu.VMEM((depth, slots, 8 * step_row), jnp.bfloat16),
            pltpu.VMEM((depth, len(PHASES), slots, 2 * slots), jnp.float32),
            pltpu.VMEM((depth, slots, slots), jnp.float32),
            pltpu.SemaphoreType.DMA((near,)),
            pltpu.SemaphoreType.DMA((near,)),
            pltpu.SemaphoreType.DMA((ITERS, near)),
            pltpu.SemaphoreType.DMA((ITERS, near)),
        ],
        compiler_params=pltpu.CompilerParams(
            collective_id=0, has_side_effects=True, vmem_limit_bytes=60 * 2**20
        ),
    )(counts.reshape(depth), positions.reshape(3, depth, slots), labels.reshape(depth, slots))
    return groups.reshape(labels.shape)


def solution(mesh):
    placed = (P(None, "gx", "gy", None, None), P("gx", "gy", None), P("gx", "gy", None, None))
    return jax.shard_map(
        body, mesh=mesh, in_specs=placed, out_specs=P("gx", "gy", None, None), check_vma=False
    )
```
